32 devices in a mesh: grp: 2 (over y), seq: 4 (over z), kvh: 2 (over x), own: 2 (over core).
Axes of the slice: x: 2, y: 2, z: 4, core: 2. Of those that a mesh axis runs over, the one named last changes fastest.
Arguments:
- hidden_input: bfloat16 [8192, 2880], P(('grp', 'seq', 'own'), 'kvh'), parts along dimension 0, may hold values from -6 to 6
- query_base: bfloat16 [8192, 4096], P(('grp', 'seq', 'own'), 'kvh'), parts along dimension 0, may hold values from -10 to 10
- frozen_keys: bfloat16 [8192, 512], P(('grp', 'seq', 'own'), 'kvh'), parts along dimension 0, may hold values from -6 to 6
- frozen_values: bfloat16 [8192, 512], P(('grp', 'seq', 'own'), 'kvh'), parts along dimension 0, may hold values from -6 to 6
- attended_gradient: bfloat16 [8192, 4096], P(('grp', 'seq', 'own'), 'kvh'), parts along dimension 0, may hold values from -6 to 6
- tenant_ids: int32 [8192, 1], P(('grp', 'seq', 'own')), parts along dimension 0, may hold values from 0 to 15; in each aligned block of 512 rows (0 to 511, 512 to 1023, ...) at most 96 rows name the same one
- doc_start: int32 [8192], P(('grp', 'seq', 'own')), parts along dimension 0, may hold values from 0 to 4095, as said below
- a_query: bfloat16 [32, 2880, 16], P(('grp', 'seq', 'own'), 'kvh'), parts along dimension 0, may hold values from -0.109375 to 0.109375
- b_query: bfloat16 [32, 16, 4096], P(('grp', 'seq', 'own'), None, 'kvh'), parts along dimension 0, may hold values from -1.5 to 1.5
- a_value: bfloat16 [32, 2880, 16], P(('grp', 'seq', 'own'), 'kvh'), parts along dimension 0, may hold values from -0.109375 to 0.109375
- value_up_factor: bfloat16 [32, 16, 512], P(('grp', 'seq', 'own'), None, 'kvh'), parts along dimension 0, may hold values from -1.5 to 1.5
Outputs:
- attended: bfloat16 [8192, 4096], P(('grp', 'seq', 'own'), 'kvh'), parts along dimension 0
- grad_a_query: float32 [32, 2880, 16], P(('grp', 'seq', 'own'), 'kvh'), parts along dimension 0
- grad_b_query: float32 [32, 16, 4096], P(('grp', 'seq', 'own'), None, 'kvh'), parts along dimension 0
- grad_a_value: float32 [32, 2880, 16], P(('grp', 'seq', 'own'), 'kvh'), parts along dimension 0
- grad_b_value: float32 [32, 16, 512], P(('grp', 'seq', 'own'), None, 'kvh'), parts along dimension 0
The draws below stay inside these ranges and needn't reach their ends.
There are 2 independent parts, one for each index of `grp`. The reference program is written for one: setup_inputs(seed, part) draws one part's arguments, and reference() takes and returns one part's arrays. A program takes and returns all parts, laid end to end along the dimension named above; each array names one. Nothing has to cross between parts.
Inputs may be any that keep to these rules, and one draw needn't show every extreme that they name: tenant_ids[i, 0] is token i's tenant; among the 512 tokens of one device at most 96 belong to one tenant, and some tenant has exactly 96 there; every tenant has tokens. doc_start[i] is the position where token i's document begins: never above i, never falling with i, equal to i where a document begins, 0 at position 0; a one-token document stands at the last position.
All inputs are finite; a program needn't handle non-finite values.
Results may differ from the reference program's by a relative error of at most 0.02125.
Values may be sent and summed in bfloat16 or wider, within the bound.
No kernel may reach another device: no remote copies, remote signals or barrier semaphores. Data moves between devices by JAX's collectives and lax.ppermute only.
A program may use at most 128 MiB of HBM per device.

```python
import math
import jax
import jax.numpy as jnp
import numpy as np
from jax import lax

MODEL_WIDTH = 2880
QUERY_HEAD_COUNT = 64
KEY_VALUE_HEADS = 8
HEAD_SIZE = 64
ATTENTION_SPAN = 128
ADAPTER_RANK = 16
TOK_DEV = 512
WINDOW_TOKENS = 4096
TENANT_COUNT = 16
CAP = 96


def draw_frozen_keys(key, part):
    random_noise = jax.random.normal(jax.random.fold_in(key, 12), (WINDOW_TOKENS, KEY_VALUE_HEADS * HEAD_SIZE), jnp.float32)
    return jnp.clip(random_noise, -6.0, 6.0).astype(jnp.bfloat16)


def draw_query_base(key, part):
    random_noise = jax.random.normal(jax.random.fold_in(key, 16), (WINDOW_TOKENS, QUERY_HEAD_COUNT * HEAD_SIZE), jnp.float32)
    return jnp.clip(random_noise, -6.0, 6.0).astype(jnp.bfloat16)


def draw_doc_start(key, part):
    fresh = jax.random.randint(jax.random.fold_in(key, 21), (WINDOW_TOKENS,), 0, 2 * ATTENTION_SPAN) == 0
    places = jnp.arange(WINDOW_TOKENS, dtype=jnp.int32)
    begins = jnp.where((places == 0) | (places == WINDOW_TOKENS - 1) | fresh, places, 0)
    return lax.cummax(begins, axis=0).astype(jnp.int32)


def block_scale(key, extent, shards, low, largest):
    loudness, own = 1.0, jax.random.fold_in(key, 6)
    for axis_at, parts in shards:
        steps = jnp.exp(jax.random.uniform(jax.random.fold_in(own, axis_at), (parts,), jnp.float32, low / len(shards), largest / len(shards)))
        loudness = loudness * jnp.repeat(steps, extent[axis_at] // parts).reshape([-1 if axis == axis_at else 1 for axis in range(len(extent))])
    return loudness


def shared_out(own_key, own, number, rows, amount, top, bound, slope):
    sequence = jax.random.permutation(own_key, amount)
    crowded, common = portions_of(amount, rows * top, bound, slope, True), portions_of(amount, rows * top, bound, slope, False)
    places = jnp.arange(amount)

    def named(sizes, rotation):
        used = int((sizes > 0).sum())
        fixed = max(1, used // 4)
        passed = fixed + (places - fixed + rotation * (used - fixed)) % max(1, amount - fixed)
        return jnp.zeros((amount,), jnp.int32).at[sequence[jnp.where(places < fixed, places, passed)]].set(jnp.asarray(sizes, jnp.int32))

    sizes = jnp.where(number % 4 == 0, named(crowded, number // 4), named(common, number - number // 4 - 1))
    mixed = jax.random.permutation(jax.random.fold_in(own, 3), amount)
    donor, taker = mixed[0:amount // 2 * 2:2], mixed[1:amount // 2 * 2:2]
    room = jnp.minimum(sizes[donor] - 1, bound - sizes[taker]) // 2
    room = jnp.where((donor == sequence[0]) | (taker == sequence[0]) | (sizes[taker] == 0), 0, jnp.maximum(room, 0))
    passed = jax.random.randint(jax.random.fold_in(own, 4), (amount // 2,), 0, 1 << 20) % (room + 1)
    sizes = sizes.at[donor].add(-passed).at[taker].add(passed)
    members = jnp.searchsorted(jnp.cumsum(sizes), jnp.arange(rows * top), side="right").astype(jnp.int32)
    table = members.reshape(top, rows).T
    table = table[jax.random.permutation(jax.random.fold_in(own, 1), rows)]
    rotation = jax.random.randint(jax.random.fold_in(own, 2), (rows, 1), 0, top)
    return jnp.take_along_axis(table, (jnp.arange(top)[None, :] + rotation) % top, axis=1)


def portions_of(number_of, total, limit, skew, full):
    loads = [(1 << 20) // math.isqrt(grade ** skew) + 1 for grade in range(1, number_of + 1)]
    largest = limit if full else min(limit, max(-(-total // number_of), total * loads[0] // sum(loads)))
    least = 1 if total - largest >= number_of - 1 else 0
    holding, spare = [largest] + [least] * (number_of - 1), total - largest - least * (number_of - 1)
    while spare > 0:
        movable = [i for i in range(1, number_of) if holding[i] < largest] or [i for i in range(1, number_of) if holding[i] < limit]
        mass, remaining = sum([loads[i] for i in movable]), spare
        for i in movable:
            extra = min(limit - holding[i], max(1, remaining * loads[i] // mass), spare)
            holding[i] = holding[i] + extra
            spare = spare - extra
    return np.array(holding)


def normal_values(own_key, shape, deviation, most, cuts=(), kind=jnp.bfloat16):
    values = jax.random.normal(own_key, shape, jnp.float32) * deviation
    if len(cuts) > 0:
        values = block_scale(own_key, shape, cuts, -0.22, 0.18) * values
    return jnp.clip(values, min=-most, max=most).astype(kind)


def setup_inputs(seed: int = 0, part: int = 0) -> dict:
    streams_of = jax.random.split(jax.random.key(seed), 12)
    own_keys = jax.random.split(jax.random.fold_in(streams_of[11], part), 12)
    hidden_input = normal_values(own_keys[0], (WINDOW_TOKENS, MODEL_WIDTH), 1.0, 6.0, ((0, 8), (1, 2)))
    query_base = draw_query_base(jax.random.fold_in(jax.random.fold_in(streams_of[11], part), 71), part)
    frozen_keys = draw_frozen_keys(jax.random.fold_in(jax.random.fold_in(streams_of[11], part), 71), part)
    frozen_values = normal_values(own_keys[3], (WINDOW_TOKENS, KEY_VALUE_HEADS * HEAD_SIZE), 1.0, 6.0, ((0, 8), (1, 2)))
    attended_gradient = normal_values(own_keys[4], (WINDOW_TOKENS, QUERY_HEAD_COUNT * HEAD_SIZE), 1.0, 6.0, ((0, 8), (1, 2)))
    tenant_ids_keys = jax.random.split(jax.random.fold_in(own_keys[5], 1), WINDOW_TOKENS // TOK_DEV)
    tenant_ids_turns = jax.random.permutation(jax.random.fold_in(own_keys[5], 3), WINDOW_TOKENS // TOK_DEV)
    tenant_ids = jax.vmap(lambda own, number: shared_out(jax.random.fold_in(own_keys[5], 2), own, number, TOK_DEV, TENANT_COUNT, 1, CAP, 2))(tenant_ids_keys, tenant_ids_turns).reshape((WINDOW_TOKENS, 1))
    doc_start = draw_doc_start(jax.random.fold_in(jax.random.fold_in(streams_of[11], part), 71), part)
    a_query = normal_values(own_keys[7], (TENANT_COUNT, MODEL_WIDTH, ADAPTER_RANK), MODEL_WIDTH ** -0.5, 0.109375, ((0, 8), (1, 2)))
    b_query = normal_values(own_keys[8], (TENANT_COUNT, ADAPTER_RANK, QUERY_HEAD_COUNT * HEAD_SIZE), ADAPTER_RANK ** -0.5, 1.5, ((0, 8), (2, 2)))
    a_value = normal_values(own_keys[9], (TENANT_COUNT, MODEL_WIDTH, ADAPTER_RANK), MODEL_WIDTH ** -0.5, 0.109375, ((0, 8), (1, 2)))
    value_up_factor = normal_values(own_keys[10], (TENANT_COUNT, ADAPTER_RANK, KEY_VALUE_HEADS * HEAD_SIZE), ADAPTER_RANK ** -0.5, 1.5, ((0, 8), (2, 2)))
    return {"hidden_input": hidden_input, "query_base": query_base, "frozen_keys": frozen_keys, "frozen_values": frozen_values, "attended_gradient": attended_gradient, "tenant_ids": tenant_ids, "doc_start": doc_start, "a_query": a_query, "b_query": b_query, "a_value": a_value, "value_up_factor": value_up_factor}


def reference(hidden_input, query_base, frozen_keys, frozen_values, attended_gradient, tenant_ids, doc_start, a_query, b_query, a_value, value_up_factor):
    single_float = jnp.float32
    brain_float_half = jnp.bfloat16
    head_group = QUERY_HEAD_COUNT // KEY_VALUE_HEADS
    scale = 1.0 / math.sqrt(HEAD_SIZE)
    count_blocks = WINDOW_TOKENS // ATTENTION_SPAN
    flat_tenants = tenant_ids[:, 0]
    a_both = jnp.concatenate([a_query, a_value], axis=2)

    def forward_block(packed_rows):
        hidden_blk, tenant_blk = packed_rows
        tenant_codes = jnp.einsum('td,tdr->tr', hidden_blk.astype(single_float), a_both[tenant_blk].astype(single_float)).astype(brain_float_half)
        delta_query = jnp.einsum('tr,trq->tq', tenant_codes[:, :ADAPTER_RANK].astype(single_float), b_query[tenant_blk].astype(single_float)).astype(brain_float_half)
        value_update = jnp.einsum('tr,trq->tq', tenant_codes[:, ADAPTER_RANK:].astype(single_float), value_up_factor[tenant_blk].astype(single_float)).astype(brain_float_half)
        return (tenant_codes, delta_query, value_update)
    tenant_codes, delta_query, value_update = lax.map(forward_block, (hidden_input.reshape(count_blocks, ATTENTION_SPAN, MODEL_WIDTH), flat_tenants.reshape(count_blocks, ATTENTION_SPAN)))
    tenant_codes = tenant_codes.reshape(WINDOW_TOKENS, 2 * ADAPTER_RANK)
    query_rows = (query_base.astype(single_float) + delta_query.reshape(WINDOW_TOKENS, QUERY_HEAD_COUNT * HEAD_SIZE).astype(single_float)).astype(brain_float_half)
    value_rows = (frozen_values.astype(single_float) + value_update.reshape(WINDOW_TOKENS, KEY_VALUE_HEADS * HEAD_SIZE).astype(single_float)).astype(brain_float_half)
    padded_keys = jnp.concatenate([jnp.zeros((ATTENTION_SPAN, KEY_VALUE_HEADS * HEAD_SIZE), brain_float_half), frozen_keys], axis=0)
    padded_values = jnp.concatenate([jnp.zeros((ATTENTION_SPAN, KEY_VALUE_HEADS * HEAD_SIZE), brain_float_half), value_rows], axis=0)

    def attend_block(block_id):
        first_entry = (block_id * ATTENTION_SPAN).astype(jnp.int32)
        query_block = lax.dynamic_slice_in_dim(query_rows, first_entry, ATTENTION_SPAN, 0).reshape(ATTENTION_SPAN, KEY_VALUE_HEADS, head_group, HEAD_SIZE).astype(single_float)
        gradient_block = lax.dynamic_slice_in_dim(attended_gradient, first_entry, ATTENTION_SPAN, 0).reshape(ATTENTION_SPAN, KEY_VALUE_HEADS, head_group, HEAD_SIZE)
        key_block = lax.dynamic_slice_in_dim(padded_keys, first_entry, 2 * ATTENTION_SPAN, 0).reshape(2 * ATTENTION_SPAN, KEY_VALUE_HEADS, HEAD_SIZE).astype(single_float)
        value_block = lax.dynamic_slice_in_dim(padded_values, first_entry, 2 * ATTENTION_SPAN, 0).reshape(2 * ATTENTION_SPAN, KEY_VALUE_HEADS, HEAD_SIZE)
        starts = lax.dynamic_slice_in_dim(doc_start, first_entry, ATTENTION_SPAN, 0)
        query_pos = first_entry + jnp.arange(ATTENTION_SPAN, dtype=jnp.int32)
        key_pos = first_entry - ATTENTION_SPAN + jnp.arange(2 * ATTENTION_SPAN, dtype=jnp.int32)
        visible = (key_pos[None, :] <= query_pos[:, None]) & (query_pos[:, None] - key_pos[None, :] < ATTENTION_SPAN) & (key_pos[None, :] >= starts[:, None])
        scores = jnp.einsum('tkgd,skd->kgts', query_block, key_block) * scale
        scores = jnp.where(visible[None, None], scores, -1e+30)
        peak = lax.optimization_barrier(jnp.max(scores, axis=-1, keepdims=True))
        expo = jnp.exp(scores - peak)
        weights = expo / lax.optimization_barrier(jnp.sum(expo, axis=-1, keepdims=True))
        weights_bf = weights.astype(brain_float_half)
        attended_block = jnp.einsum('kgts,skd->tkgd', weights_bf.astype(single_float), value_block.astype(single_float)).astype(brain_float_half)
        row_term = lax.optimization_barrier(jnp.sum(gradient_block.astype(single_float) * attended_block.astype(single_float), axis=-1))
        grad_weights = jnp.einsum('tkgd,skd->kgts', gradient_block.astype(single_float), value_block.astype(single_float))
        grad_scores = weights * (grad_weights - jnp.transpose(row_term, (1, 2, 0))[..., None])
        grad_scores_bf = grad_scores.astype(brain_float_half)
        query_gradient = jnp.einsum('kgts,skd->tkgd', grad_scores_bf.astype(single_float), key_block) * scale
        key_gradient = jnp.einsum('kgts,tkgd->skd', weights_bf.astype(single_float), gradient_block.astype(single_float))
        return (attended_block.reshape(ATTENTION_SPAN, QUERY_HEAD_COUNT * HEAD_SIZE), query_gradient.reshape(ATTENTION_SPAN, QUERY_HEAD_COUNT * HEAD_SIZE), key_gradient.reshape(2 * ATTENTION_SPAN, KEY_VALUE_HEADS * HEAD_SIZE))
    attended, query_gradient, key_gradient = lax.map(attend_block, jnp.arange(count_blocks, dtype=jnp.int32))
    attended = attended.reshape(WINDOW_TOKENS, QUERY_HEAD_COUNT * HEAD_SIZE)
    query_gradient = query_gradient.reshape(WINDOW_TOKENS, QUERY_HEAD_COUNT * HEAD_SIZE).astype(brain_float_half)
    later_rows = jnp.concatenate([key_gradient[1:, :ATTENTION_SPAN], jnp.zeros((1, ATTENTION_SPAN, KEY_VALUE_HEADS * HEAD_SIZE), single_float)], axis=0)
    value_gradient = (key_gradient[:, ATTENTION_SPAN:] + later_rows).reshape(WINDOW_TOKENS, KEY_VALUE_HEADS * HEAD_SIZE).astype(brain_float_half)

    def back_step(carry, packed_rows):
        acc_a, acc_bq, acc_bv = carry
        hidden_blk, tenant_blk, codes_blk, gq_blk, gv_blk = packed_rows
        factor = jnp.concatenate([jnp.einsum('tq,trq->tr', gq_blk.astype(single_float), b_query[tenant_blk].astype(single_float)), jnp.einsum('tq,trq->tr', gv_blk.astype(single_float), value_up_factor[tenant_blk].astype(single_float))], axis=1).astype(brain_float_half)
        acc_a = acc_a + jax.ops.segment_sum(hidden_blk.astype(single_float)[:, :, None] * factor.astype(single_float)[:, None, :], tenant_blk, num_segments=TENANT_COUNT)
        acc_bq = acc_bq + jax.ops.segment_sum(codes_blk[:, :ADAPTER_RANK].astype(single_float)[:, :, None] * gq_blk.astype(single_float)[:, None, :], tenant_blk, num_segments=TENANT_COUNT)
        acc_bv = acc_bv + jax.ops.segment_sum(codes_blk[:, ADAPTER_RANK:].astype(single_float)[:, :, None] * gv_blk.astype(single_float)[:, None, :], tenant_blk, num_segments=TENANT_COUNT)
        return ((acc_a, acc_bq, acc_bv), None)
    initial_accumulator = (jnp.zeros((TENANT_COUNT, MODEL_WIDTH, 2 * ADAPTER_RANK), single_float), jnp.zeros((TENANT_COUNT, ADAPTER_RANK, QUERY_HEAD_COUNT * HEAD_SIZE), single_float), jnp.zeros((TENANT_COUNT, ADAPTER_RANK, KEY_VALUE_HEADS * HEAD_SIZE), single_float))
    packed_rows = (hidden_input.reshape(count_blocks, ATTENTION_SPAN, MODEL_WIDTH), flat_tenants.reshape(count_blocks, ATTENTION_SPAN), tenant_codes.reshape(count_blocks, ATTENTION_SPAN, 2 * ADAPTER_RANK), query_gradient.reshape(count_blocks, ATTENTION_SPAN, QUERY_HEAD_COUNT * HEAD_SIZE), value_gradient.reshape(count_blocks, ATTENTION_SPAN, KEY_VALUE_HEADS * HEAD_SIZE))
    (acc_a, acc_bq, acc_bv), unused = lax.scan(back_step, initial_accumulator, packed_rows)
    return (attended, acc_a[:, :, :ADAPTER_RANK], acc_bq, acc_a[:, :, ADAPTER_RANK:], acc_bv)
```

```python
import math

import jax
import jax.numpy as jnp
from jax import lax
from jax.experimental import pallas as pl
from jax.experimental.pallas import tpu as pltpu
from jax.sharding import PartitionSpec as P

HEAD_SIZE = 64
ATTENTION_SPAN = 128
LANES = 128
F32 = jnp.float32
BF16 = jnp.bfloat16
NT = (((1,), (1,)), ((), ()))
VMEM_LIMIT = 60 * 1024 * 1024
LOG2E = 1.4426950408889634


def vmem():
    return pl.BlockSpec(memory_space=pltpu.VMEM)


def smem():
    return pl.BlockSpec(memory_space=pltpu.SMEM)


def params(**more):
    return pltpu.CompilerParams(vmem_limit_bytes=VMEM_LIMIT, **more)


def rotate(block, axis, by):
    size = lax.axis_size(axis)
    return lax.ppermute(block, axis, [(i, (i + by) % size) for i in range(size)])


def rotate_two(block, by_kvh, by_own):
    nk, no = lax.axis_size("kvh"), lax.axis_size("own")
    pairs = [
        (k * no + o, ((k + by_kvh) % nk) * no + (o + by_own) % no)
        for k in range(nk)
        for o in range(no)
    ]
    return lax.ppermute(block, ("kvh", "own"), pairs)


def shifted(shard, axis, by):
    peers = lax.axis_size(axis)
    pairs = [(i, i + by) for i in range(peers) if 0 <= i + by < peers]
    return lax.ppermute(shard, axis, pairs)


def codes_kernel(pieces, sets, table, *refs):
    a_refs, refs = refs[:pieces], refs[pieces:]
    h_refs, refs = refs[:sets], refs[sets:]
    id_refs, out_refs = refs[:sets], refs[sets:]
    both = out_refs[0].shape[0]
    factors = jnp.concatenate([a[...] for a in a_refs], axis=0)
    tenants = factors.shape[0] // both
    for n in range(sets):
        codes = jnp.dot(factors, h_refs[n][...], preferred_element_type=F32)
        ids = id_refs[n][...]
        total = jnp.zeros(out_refs[n].shape, F32)
        for j in range(tenants):
            mine = codes[j * both : (j + 1) * both]
            total = total + jnp.where(ids == table[j], mine, 0.0)
        out_refs[n][...] = total


def spread_kernel(parts, table, *refs):
    part_refs, refs = refs[:parts], refs[parts:]
    ids_ref, up_ref, frozen_ref, value_ref, rows_ref, etq_ref, etv_ref = refs
    total = part_refs[0][...]
    for n in range(1, parts):
        total = total + part_refs[n][...]
    rank = total.shape[0] // 2
    tenants = etq_ref.shape[0] // rank
    codes = total.astype(BF16).astype(F32)
    ids = ids_ref[...]
    wide_q, wide_v = [], []
    for j in range(tenants):
        hit = ids == table[j]
        wide_q.append(jnp.where(hit, codes[:rank], 0.0))
        wide_v.append(jnp.where(hit, codes[rank:], 0.0))
    wide_q = jnp.concatenate(wide_q, axis=0)
    wide_v = jnp.concatenate(wide_v, axis=0)
    etq_ref[...] = wide_q.astype(BF16)
    etv_ref[...] = wide_v.astype(BF16)
    rows_ref[...] = wide_q.T.astype(BF16)
    update = jnp.dot(wide_v.T.astype(BF16), up_ref[...], preferred_element_type=F32)
    value_ref[...] = (frozen_ref[...].astype(F32) + update.astype(BF16).astype(F32)).astype(BF16)


def attention_kernel(
    kv_heads, group, base, q_ref, g_ref, e_ref, b_ref, k_ref, v_ref, d_ref, o_ref, dq_ref, dv_ref
):
    block = pl.program_id(0)
    rows = q_ref.shape[0]
    span = rows + ATTENTION_SPAN
    first = pl.multiple_of(block * rows, rows)
    window = pl.ds(first, span)

    @pl.when(block == 0)
    def _():
        dv_ref[...] = jnp.zeros_like(dv_ref)

    slot = lax.broadcasted_iota(jnp.int32, (rows, rows), 0)
    token = lax.broadcasted_iota(jnp.int32, (rows, rows), 1)
    current = slot <= token
    position = base[0] + first + slot - jnp.where(current, 0, ATTENTION_SPAN)
    bias = jnp.where(position >= d_ref[...], 0.0, -1e30).astype(F32)
    current = jnp.concatenate([current, current], axis=1)
    bias = jnp.concatenate([bias, bias], axis=1)
    now = jnp.where(current, 1.0, 0.0).astype(BF16)
    before = jnp.where(current, 0.0, 1.0).astype(BF16)
    low = lax.broadcasted_iota(jnp.int32, (span, LANES), 1) < HEAD_SIZE
    factor = LOG2E / math.sqrt(HEAD_SIZE)
    scale = 1.0 / math.sqrt(HEAD_SIZE)
    width = group * HEAD_SIZE
    quads = max(1, width // (2 * LANES))

    for pair in range(k_ref.shape[1] // LANES):
        lanes = slice(pair * LANES, (pair + 1) * LANES)
        k_pair = k_ref[window, lanes].astype(F32)
        v_pair = v_ref[window, lanes].astype(F32)
        k_turned = k_pair.T.astype(BF16)
        v_turned = v_pair.T.astype(BF16)
        dv_pair = jnp.zeros((span, LANES), F32)
        for half in range(2):
            g = pair * 2 + half
            if g >= kv_heads:
                continue
            if half == 0:
                k_low, v_low = jnp.where(low, k_pair, 0.0), jnp.where(low, v_pair, 0.0)
                k_high, v_high = pltpu.roll(k_low, HEAD_SIZE, 1), pltpu.roll(v_low, HEAD_SIZE, 1)
            else:
                k_high, v_high = jnp.where(low, 0.0, k_pair), jnp.where(low, 0.0, v_pair)
                k_low, v_low = pltpu.roll(k_high, HEAD_SIZE, 1), pltpu.roll(v_high, HEAD_SIZE, 1)
            k_both = jnp.concatenate([k_low, k_high], axis=0).astype(BF16)
            v_both = jnp.concatenate([v_low, v_high], axis=0).astype(BF16)
            k_t = k_turned[half * HEAD_SIZE : (half + 1) * HEAD_SIZE]
            v_t = v_turned[half * HEAD_SIZE : (half + 1) * HEAD_SIZE]
            columns = slice(g * width, (g + 1) * width)
            delta = jnp.dot(e_ref[...], b_ref[:, columns], preferred_element_type=F32)
            query = (q_ref[:, columns].astype(F32) + delta.astype(BF16).astype(F32)).astype(BF16)
            dv_heads = [jnp.zeros((span, LANES), F32), jnp.zeros((span, LANES), F32)]
            for quad in range(quads):
                at = quad * 2 * LANES
                here = g * width + at
                qq = jnp.concatenate(
                    [query[:, at : at + LANES], query[:, at + LANES : at + 2 * LANES]], axis=0
                )
                gg = jnp.concatenate(
                    [g_ref[:, here : here + LANES], g_ref[:, here + LANES : here + 2 * LANES]],
                    axis=0,
                )
                scores = lax.dot_general(k_both, qq, NT, preferred_element_type=F32)
                dps = lax.dot_general(v_both, gg, NT, preferred_element_type=F32)
                out_t, dq_t = [], []
                for head in range(2):
                    top = head * span
                    mid = top + ATTENTION_SPAN
                    end = top + span
                    s = jnp.where(current, scores[mid:end], scores[top:mid]) + bias
                    peak = jnp.max(s, axis=0, keepdims=True)
                    expo = jnp.exp2((s - peak) * factor)
                    weights = expo * (1.0 / jnp.sum(expo, axis=0, keepdims=True))
                    dp = jnp.where(current, dps[mid:end], dps[top:mid])
                    row_term = jnp.sum(weights * dp, axis=0, keepdims=True)
                    ds = (weights * (dp - row_term)).astype(BF16)
                    weights = weights.astype(BF16)
                    w_wide = jnp.concatenate([weights * before, weights * now], axis=0)
                    ds_wide = jnp.concatenate([ds * before, ds * now], axis=0)
                    out_t.append(jnp.dot(v_t, w_wide, preferred_element_type=F32))
                    dq_t.append(jnp.dot(k_t, ds_wide, preferred_element_type=F32) * scale)
                    dv_heads[head] = dv_heads[head] + jnp.dot(
                        w_wide, gg, preferred_element_type=F32
                    )
                out_t = jnp.concatenate(out_t, axis=0)
                dq_t = jnp.concatenate(dq_t, axis=0)
                for n in range(2):
                    put = slice(here + n * LANES, here + (n + 1) * LANES)
                    take = slice(n * rows, (n + 1) * rows)
                    o_ref[:, put] = out_t[:, take].T.astype(BF16)
                    dq_ref[:, put] = dq_t[:, take].T.astype(BF16)
            first_part = jnp.where(low, dv_heads[0], 0.0)
            second_part = jnp.where(low, 0.0, dv_heads[1])
            if half == 0:
                dv_pair = dv_pair + first_part + pltpu.roll(second_part, HEAD_SIZE, 1)
            else:
                dv_pair = dv_pair + second_part + pltpu.roll(first_part, HEAD_SIZE, 1)
        dv_ref[window, lanes] = dv_ref[window, lanes] + dv_pair


def products_kernel(
    rank, table, ids_ref, etq_ref, etv_ref, dq_ref, gv_ref, bq_ref, bv_ref, gq_out, gv_out, f_out, acc
):
    step = pl.program_id(0)

    @pl.when(step == 0)
    def _():
        acc[...] = jnp.zeros_like(acc)
        gv_out[...] = jnp.dot(etv_ref[...], gv_ref[...], preferred_element_type=F32).astype(BF16)

    gq_out[...] = jnp.dot(etq_ref[...], dq_ref[...], preferred_element_type=F32).astype(BF16)
    acc[...] += lax.dot_general(bq_ref[...], dq_ref[...], NT, preferred_element_type=F32)

    @pl.when(step == pl.num_programs(0) - 1)
    def _():
        wide_v = lax.dot_general(bv_ref[...], gv_ref[...], NT, preferred_element_type=F32)
        ids = ids_ref[...]
        total_q = jnp.zeros((rank, ids.shape[1]), F32)
        total_v = jnp.zeros((rank, ids.shape[1]), F32)
        for j in range(acc.shape[0] // rank):
            hit = ids == table[j]
            total_q = total_q + jnp.where(hit, acc[j * rank : (j + 1) * rank], 0.0)
            total_v = total_v + jnp.where(hit, wide_v[j * rank : (j + 1) * rank], 0.0)
        f_out[...] = jnp.concatenate([total_q, total_v], axis=0)


def outer_kernel(sets, parts, pieces, table, *refs):
    f_refs, refs = refs[: sets * parts], refs[sets * parts :]
    id_refs, refs = refs[:sets], refs[sets:]
    h_refs, out_refs = refs[:sets], refs[sets:]
    both = f_refs[0].shape[0]
    each = out_refs[0].shape[0] // both
    total = None
    for n in range(sets):
        factor = f_refs[n * parts][...]
        for k in range(1, parts):
            factor = factor + f_refs[n * parts + k][...]
        ids = id_refs[n][...]
        wide = jnp.concatenate(
            [jnp.where(ids == table[j], factor, 0.0).astype(BF16) for j in range(pieces * each)],
            axis=0,
        )
        term = lax.dot_general(wide, h_refs[n][...], NT, preferred_element_type=F32)
        total = term if total is None else total + term
    high = out_refs[0].shape[0]
    for p in range(pieces):
        out_refs[p][...] = total[p * high : (p + 1) * high].astype(BF16)


def body(
    hidden_input,
    query_base,
    frozen_keys,
    frozen_values,
    attended_gradient,
    tenant_ids,
    doc_start,
    a_query,
    b_query,
    a_value,
    value_up_factor,
):
    rows_dev, width = hidden_input.shape
    query_width = query_base.shape[1]
    kv_width = frozen_keys.shape[1]
    local, _, rank = a_query.shape
    both = 2 * rank
    ns, nk, no = lax.axis_size("seq"), lax.axis_size("kvh"), lax.axis_size("own")
    seq_at, own_at = lax.axis_index("seq"), lax.axis_index("own")
    kv_heads = kv_width // HEAD_SIZE
    group = query_width // kv_width

    hops = jnp.arange(ns, dtype=jnp.int32)
    turns = jnp.arange(no, dtype=jnp.int32)
    seq_of = (seq_at - hops) % ns
    own_of = (own_at - turns) % no
    table = (
        (seq_of[None, :, None] * no + own_of[:, None, None]) * local
        + jnp.arange(local, dtype=jnp.int32)[None, None, :]
    ).astype(jnp.int32)
    table_all = table.reshape(-1)
    table_own = table[0].reshape(-1)

    hidden_t = hidden_input.T
    ids = tenant_ids.reshape(1, rows_dev)
    hidden_sets = [hidden_t] + [rotate(hidden_t, "own", d) for d in range(1, no)]
    id_sets = [ids] + [rotate(ids, "own", d) for d in range(1, no)]

    a_own = jnp.concatenate([a_query.swapaxes(1, 2), a_value.swapaxes(1, 2)], axis=1).reshape(
        local * both, width
    )
    a_pieces = [a_own] + [rotate(a_own, "seq", k) for k in range(1, ns)]

    code_parts = pl.pallas_call(
        lambda *refs: codes_kernel(ns, no, *refs),
        out_shape=[jax.ShapeDtypeStruct((both, rows_dev), F32)] * no,
        in_specs=[smem()] + [vmem()] * (ns + 2 * no),
        out_specs=[vmem()] * no,
        compiler_params=params(),
        name="codes",
    )(table_own, *a_pieces, *hidden_sets, *id_sets)

    parts = [code_parts[0]]
    for dk in range(nk):
        for d in range(no):
            if dk or d:
                parts.append(rotate_two(code_parts[(-d) % no], dk, d))

    b_own = jnp.concatenate([b_query, value_up_factor], axis=2).reshape(
        local * rank, query_width + kv_width
    )
    b_seq = jnp.concatenate([b_own] + [rotate(b_own, "seq", k) for k in range(1, ns)], axis=0)
    b_all = jnp.concatenate([b_seq] + [rotate(b_seq, "own", d) for d in range(1, no)], axis=0)
    up_query = b_all[:, :query_width]
    up_value = b_all[:, query_width:]
    wide = b_all.shape[0]

    value_new, rows_q, et_query, et_value = pl.pallas_call(
        lambda *refs: spread_kernel(nk * no, *refs),
        out_shape=[
            jax.ShapeDtypeStruct((rows_dev, kv_width), BF16),
            jax.ShapeDtypeStruct((rows_dev, wide), BF16),
            jax.ShapeDtypeStruct((wide, rows_dev), BF16),
            jax.ShapeDtypeStruct((wide, rows_dev), BF16),
        ],
        in_specs=[smem()] + [vmem()] * (nk * no + 3),
        out_specs=[vmem()] * 4,
        compiler_params=params(),
        name="spread",
    )(table_all, *parts, ids, up_value, frozen_values)

    tail = jnp.concatenate(
        [frozen_keys[rows_dev - ATTENTION_SPAN :], value_new[rows_dev - ATTENTION_SPAN :]], axis=1
    )
    rim = shifted(tail, ("seq", "own"), 1)
    key_full = jnp.concatenate([rim[:, :kv_width], frozen_keys], axis=0)
    value_full = jnp.concatenate([rim[:, kv_width:], value_new], axis=0)
    lane_gap = (-kv_width) % LANES
    if lane_gap:
        key_full = jnp.pad(key_full, ((0, 0), (0, lane_gap)))
        value_full = jnp.pad(value_full, ((0, 0), (0, lane_gap)))
    full_rows, full_width = key_full.shape
    block = ATTENTION_SPAN
    my_index = seq_at * no + own_at
    base = (my_index * rows_dev).astype(jnp.int32).reshape(1)

    def whole(shape):
        return pl.BlockSpec(shape, lambda i: (0, 0))

    def by_rows(columns):
        return pl.BlockSpec((block, columns), lambda i: (i, 0))

    attended, query_grad, value_grad = pl.pallas_call(
        lambda *refs: attention_kernel(kv_heads, group, *refs),
        grid=(rows_dev // block,),
        out_shape=[
            jax.ShapeDtypeStruct((rows_dev, query_width), BF16),
            jax.ShapeDtypeStruct((rows_dev, query_width), BF16),
            jax.ShapeDtypeStruct((full_rows, full_width), F32),
        ],
        in_specs=[
            smem(),
            by_rows(query_width),
            by_rows(query_width),
            by_rows(wide),
            whole((wide, query_width)),
            whole((full_rows, full_width)),
            whole((full_rows, full_width)),
            pl.BlockSpec((1, block), lambda i: (0, i)),
        ],
        out_specs=[by_rows(query_width), by_rows(query_width), whole((full_rows, full_width))],
        compiler_params=params(dimension_semantics=("arbitrary",)),
        name="attention",
    )(
        base,
        query_base,
        attended_gradient,
        rows_q,
        up_query,
        key_full,
        value_full,
        doc_start.reshape(1, rows_dev),
    )

    value_grad = value_grad[:, :kv_width]
    rim_back = shifted(value_grad[:ATTENTION_SPAN].astype(BF16), ("seq", "own"), -1)
    value_total = jnp.concatenate(
        [
            value_grad[ATTENTION_SPAN:rows_dev],
            value_grad[rows_dev:] + rim_back.astype(F32),
        ],
        axis=0,
    ).astype(BF16)

    chunk = min(512, query_width)
    grad_up_query, grad_up_value, factor_own = pl.pallas_call(
        lambda *refs: products_kernel(rank, *refs),
        grid=(query_width // chunk,),
        out_shape=[
            jax.ShapeDtypeStruct((wide, query_width), BF16),
            jax.ShapeDtypeStruct((wide, kv_width), BF16),
            jax.ShapeDtypeStruct((both, rows_dev), F32),
        ],
        in_specs=[
            smem(),
            whole((1, rows_dev)),
            whole((wide, rows_dev)),
            whole((wide, rows_dev)),
            pl.BlockSpec((rows_dev, chunk), lambda i: (0, i)),
            whole((rows_dev, kv_width)),
            pl.BlockSpec((wide, chunk), lambda i: (0, i)),
            whole((wide, kv_width)),
        ],
        out_specs=[
            pl.BlockSpec((wide, chunk), lambda i: (0, i)),
            whole((wide, kv_width)),
            whole((both, rows_dev)),
        ],
        scratch_shapes=[pltpu.VMEM((wide, rows_dev), F32)],
        compiler_params=params(dimension_semantics=("arbitrary",)),
        name="products",
    )(table_all, ids, et_query, et_value, query_grad, value_total, up_query, up_value)

    factors = []
    for d in range(no):
        for dk in range(nk):
            factors.append(rotate_two(factor_own, dk, d) if dk or d else factor_own)

    outer_parts = pl.pallas_call(
        lambda *refs: outer_kernel(no, nk, ns, *refs),
        out_shape=[jax.ShapeDtypeStruct((local * both, width), BF16)] * ns,
        in_specs=[smem()] + [vmem()] * (no * nk + 2 * no),
        out_specs=[vmem()] * ns,
        compiler_params=params(),
        name="outer",
    )(table_own, *factors, *id_sets, *hidden_sets)
    grad_a = outer_parts[0].astype(F32)
    for k in range(1, ns):
        grad_a = grad_a + rotate(outer_parts[k], "seq", -k).astype(F32)
    grad_a = grad_a.reshape(local, both, width)

    grad_up = jnp.concatenate([grad_up_query, grad_up_value], axis=1)
    each = wide // no
    mine = grad_up[:each].astype(F32)
    for d in range(1, no):
        mine = mine + rotate(grad_up[d * each : (d + 1) * each], "own", -d).astype(F32)
    mine = mine.astype(BF16).reshape(ns, local * rank, query_width + kv_width)
    grad_b = mine[0].astype(F32)
    for k in range(1, ns):
        grad_b = grad_b + rotate(mine[k], "seq", -k).astype(F32)
    grad_b = grad_b.reshape(local, rank, query_width + kv_width)
    return (
        attended,
        grad_a[:, :rank].swapaxes(1, 2),
        grad_b[:, :, :query_width],
        grad_a[:, rank:].swapaxes(1, 2),
        grad_b[:, :, query_width:],
    )


def solution(mesh):
    rows = ("grp", "seq", "own")
    in_specs = (
        P(rows, "kvh"),
        P(rows, "kvh"),
        P(rows, "kvh"),
        P(rows, "kvh"),
        P(rows, "kvh"),
        P(rows, None),
        P(rows),
        P(rows, "kvh", None),
        P(rows, None, "kvh"),
        P(rows, "kvh", None),
        P(rows, None, "kvh"),
    )
    out_specs = (
        P(rows, "kvh"),
        P(rows, "kvh", None),
        P(rows, None, "kvh"),
        P(rows, "kvh", None),
        P(rows, None, "kvh"),
    )
    return jax.shard_map(body, mesh=mesh, in_specs=in_specs, out_specs=out_specs, check_vma=False)
```

```python
import math

import jax
import jax.numpy as jnp
from jax import lax
from jax.experimental import pallas as pl
from jax.experimental.pallas import tpu as pltpu
from jax.sharding import PartitionSpec as P

HEAD_SIZE = 64
ATTENTION_SPAN = 128
LANES = 128
F32 = jnp.float32
BF16 = jnp.bfloat16
NT = (((1,), (1,)), ((), ()))
LOG2E = 1.4426950408889634


def vmem():
    return pl.BlockSpec(memory_space=pltpu.VMEM)


def smem():
    return pl.BlockSpec(memory_space=pltpu.SMEM)


def params(mebibytes, **more):
    return pltpu.CompilerParams(vmem_limit_bytes=mebibytes * 1024 * 1024, **more)


def after(values, *others):
    return lax.optimization_barrier((values, others))[0]


def rotate(block, axis, by):
    size = lax.axis_size(axis)
    return lax.ppermute(block, axis, [(i, (i + by) % size) for i in range(size)])


def rotate_two(block, by_kvh, by_own):
    nk, no = lax.axis_size("kvh"), lax.axis_size("own")
    pairs = [
        (k * no + o, ((k + by_kvh) % nk) * no + (o + by_own) % no)
        for k in range(nk)
        for o in range(no)
    ]
    return lax.ppermute(block, ("kvh", "own"), pairs)


def shifted(shard, axis, by):
    peers = lax.axis_size(axis)
    pairs = [(i, i + by) for i in range(peers) if 0 <= i + by < peers]
    return lax.ppermute(shard, axis, pairs)


def tenant(j, local):
    ns, no = lax.axis_size("seq"), lax.axis_size("own")
    seq_at, own_at = lax.axis_index("seq"), lax.axis_index("own")
    row, rest = j // (ns * local), j % (ns * local)
    hop, inside = rest // local, rest % local
    seq_of = lax.rem(seq_at - hop + ns, ns)
    own_of = lax.rem(own_at - row + no, no)
    return (seq_of * no + own_of) * local + inside


def codes_kernel(pieces, sets, local, *refs):
    a_refs, refs = refs[:pieces], refs[pieces:]
    h_refs, refs = refs[:sets], refs[sets:]
    id_refs, out_refs = refs[:sets], refs[sets:]
    both = out_refs[0].shape[0]
    factors = jnp.concatenate([a[...] for a in a_refs], axis=0)
    tenants = factors.shape[0] // both
    for n in range(sets):
        codes = jnp.dot(factors, h_refs[n][...], preferred_element_type=F32)
        ids = id_refs[n][...]
        total = jnp.zeros(out_refs[n].shape, F32)
        for j in range(tenants):
            mine = codes[j * both : (j + 1) * both]
            total = total + jnp.where(ids == tenant(j, local), mine, 0.0)
        out_refs[n][...] = total


def spread_kernel(parts, local, *refs):
    part_refs, refs = refs[:parts], refs[parts:]
    up_refs, refs = refs[:2], refs[2:]
    ids_ref, keys_ref, frozen_ref, value_ref, rows_ref, etq_ref, etv_ref, tail_ref, up_ref = refs
    total = part_refs[0][...]
    for n in range(1, parts):
        total = total + part_refs[n][...]
    rank = total.shape[0] // 2
    tenants = etq_ref.shape[0] // rank
    codes = total.astype(BF16).astype(F32)
    ids = ids_ref[...]
    wide_q, wide_v = [], []
    for j in range(tenants):
        hit = ids == tenant(j, local)
        wide_q.append(jnp.where(hit, codes[:rank], 0.0))
        wide_v.append(jnp.where(hit, codes[rank:], 0.0))
    wide_q = jnp.concatenate(wide_q, axis=0)
    wide_v = jnp.concatenate(wide_v, axis=0)
    etq_ref[...] = wide_q.astype(BF16)
    etv_ref[...] = wide_v.astype(BF16)
    rows_ref[...] = wide_q.T.astype(BF16)
    up = jnp.concatenate([r[...] for r in up_refs], axis=0)
    up_ref[...] = up
    update = jnp.dot(wide_v.T.astype(BF16), up, preferred_element_type=F32)
    value = (frozen_ref[...].astype(F32) + update.astype(BF16).astype(F32)).astype(BF16)
    value_ref[...] = value
    kv_width = value.shape[1]
    at = value.shape[0] - ATTENTION_SPAN
    tail_ref[:, :kv_width] = keys_ref[at:, :]
    tail_ref[:, kv_width:] = value[at:]


def heads_step(position, starts, query_of, grad_ref, key, value, pairs, kv_heads, group, put):
    rows = grad_ref.shape[0]
    span = rows + ATTENTION_SPAN
    slot = lax.broadcasted_iota(jnp.int32, (rows, rows), 0)
    token = lax.broadcasted_iota(jnp.int32, (rows, rows), 1)
    current = slot <= token
    place = position + slot - jnp.where(current, 0, ATTENTION_SPAN)
    bias = jnp.where(place >= starts, 0.0, -1e30).astype(F32)
    current = jnp.concatenate([current, current], axis=1)
    bias = jnp.concatenate([bias, bias], axis=1)
    now = jnp.where(current, 1.0, 0.0).astype(BF16)
    before = jnp.where(current, 0.0, 1.0).astype(BF16)
    low = lax.broadcasted_iota(jnp.int32, (span, LANES), 1) < HEAD_SIZE
    factor = LOG2E / math.sqrt(HEAD_SIZE)
    scale = 1.0 / math.sqrt(HEAD_SIZE)
    width = group * HEAD_SIZE
    quads = max(1, width // (2 * LANES))

    for pair in range(pairs):
        lanes = slice(pair * LANES, (pair + 1) * LANES)
        k_pair = key(lanes).astype(F32)
        v_pair = value(lanes).astype(F32)
        k_turned = k_pair.T.astype(BF16)
        v_turned = v_pair.T.astype(BF16)
        dv_pair = jnp.zeros((span, LANES), F32)
        for half in range(2):
            g = pair * 2 + half
            if g >= kv_heads:
                continue
            if half == 0:
                k_low, v_low = jnp.where(low, k_pair, 0.0), jnp.where(low, v_pair, 0.0)
                k_high, v_high = pltpu.roll(k_low, HEAD_SIZE, 1), pltpu.roll(v_low, HEAD_SIZE, 1)
            else:
                k_high, v_high = jnp.where(low, 0.0, k_pair), jnp.where(low, 0.0, v_pair)
                k_low, v_low = pltpu.roll(k_high, HEAD_SIZE, 1), pltpu.roll(v_high, HEAD_SIZE, 1)
            k_both = jnp.concatenate([k_low, k_high], axis=0).astype(BF16)
            v_both = jnp.concatenate([v_low, v_high], axis=0).astype(BF16)
            k_t = k_turned[half * HEAD_SIZE : (half + 1) * HEAD_SIZE]
            v_t = v_turned[half * HEAD_SIZE : (half + 1) * HEAD_SIZE]
            query = query_of(slice(g * width, (g + 1) * width))
            dv_heads = [jnp.zeros((span, LANES), F32), jnp.zeros((span, LANES), F32)]
            for quad in range(quads):
                at = quad * 2 * LANES
                here = g * width + at
                qq = jnp.concatenate(
                    [query[:, at : at + LANES], query[:, at + LANES : at + 2 * LANES]], axis=0
                )
                gg = jnp.concatenate(
                    [
                        grad_ref[:, here : here + LANES],
                        grad_ref[:, here + LANES : here + 2 * LANES],
                    ],
                    axis=0,
                )
                scores = lax.dot_general(k_both, qq, NT, preferred_element_type=F32)
                dps = lax.dot_general(v_both, gg, NT, preferred_element_type=F32)
                out_t, dq_t = [], []
                for head in range(2):
                    top = head * span
                    mid = top + ATTENTION_SPAN
                    end = top + span
                    s = jnp.where(current, scores[mid:end], scores[top:mid]) + bias
                    peak = jnp.max(s, axis=0, keepdims=True)
                    expo = jnp.exp2((s - peak) * factor)
                    weights = expo * (1.0 / jnp.sum(expo, axis=0, keepdims=True))
                    dp = jnp.where(current, dps[mid:end], dps[top:mid])
                    row_term = jnp.sum(weights * dp, axis=0, keepdims=True)
                    ds = (weights * (dp - row_term)).astype(BF16)
                    weights = weights.astype(BF16)
                    w_wide = jnp.concatenate([weights * before, weights * now], axis=0)
                    ds_wide = jnp.concatenate([ds * before, ds * now], axis=0)
                    out_t.append(jnp.dot(v_t, w_wide, preferred_element_type=F32))
                    dq_t.append(jnp.dot(k_t, ds_wide, preferred_element_type=F32) * scale)
                    dv_heads[head] = dv_heads[head] + jnp.dot(
                        w_wide, gg, preferred_element_type=F32
                    )
                out_t = jnp.concatenate(out_t, axis=0)
                dq_t = jnp.concatenate(dq_t, axis=0)
                for n in range(2):
                    columns = slice(here + n * LANES, here + (n + 1) * LANES)
                    take = slice(n * rows, (n + 1) * rows)
                    put("o", columns, out_t[:, take].T.astype(BF16))
                    put("dq", columns, dq_t[:, take].T.astype(BF16))
            first_part = jnp.where(low, dv_heads[0], 0.0)
            second_part = jnp.where(low, 0.0, dv_heads[1])
            if half == 0:
                dv_pair = dv_pair + first_part + pltpu.roll(second_part, HEAD_SIZE, 1)
            else:
                dv_pair = dv_pair + second_part + pltpu.roll(first_part, HEAD_SIZE, 1)
        put("dv", lanes, dv_pair)


def first_row(rows_dev):
    return (lax.axis_index("seq") * lax.axis_size("own") + lax.axis_index("own")) * rows_dev


def inner_kernel(kv_heads, group, pieces, chained, rows_dev, *refs):
    up_refs, refs = refs[:pieces], refs[pieces:]
    q_ref, g_ref, e_ref, k_ref, v_ref, d_ref = refs[:6]
    o_ref, dq_ref, dv_ref, up = refs[6 + chained :]
    step = pl.program_id(0)
    rows = q_ref.shape[0]

    @pl.when(step == 0)
    def _():
        dv_ref[...] = jnp.zeros_like(dv_ref)
        high = up_refs[0].shape[0]
        for n in range(pieces):
            up[n * high : (n + 1) * high, :] = up_refs[n][...]

    window = pl.ds(pl.multiple_of(step * rows, rows), rows + ATTENTION_SPAN)

    def query_of(columns):
        delta = jnp.dot(e_ref[...], up[:, columns], preferred_element_type=F32)
        return (q_ref[:, columns].astype(F32) + delta.astype(BF16).astype(F32)).astype(BF16)

    def put(kind, columns, block):
        if kind == "dv":
            dv_ref[window, columns] = dv_ref[window, columns] + block
        else:
            (o_ref if kind == "o" else dq_ref)[:, columns] = block

    heads_step(
        first_row(rows_dev) + (step + 1) * rows,
        d_ref[...],
        query_of,
        g_ref,
        lambda lanes: k_ref[window, lanes],
        lambda lanes: v_ref[window, lanes],
        1,
        kv_heads,
        group,
        put,
    )


def edge_kernel(kv_heads, group, chunks, pieces, rows_dev, *refs):
    up_refs, refs = refs[: chunks * pieces], refs[chunks * pieces :]
    q_ref, g_ref, e_ref, k_ref, v_ref, rim_ref, d_ref = refs[:7]
    o_ref, dq_ref, back_ref, dv_ref = refs[9:]
    rows = q_ref.shape[0]
    kv_width = kv_heads * HEAD_SIZE
    chunk = q_ref.shape[1] // chunks
    ups = [
        jnp.concatenate([r[...] for r in up_refs[c * pieces : (c + 1) * pieces]], axis=0)
        for c in range(chunks)
    ]

    def query_of(columns):
        c = columns.start // chunk
        inside = slice(columns.start - c * chunk, columns.stop - c * chunk)
        delta = jnp.dot(e_ref[...], ups[c][:, inside], preferred_element_type=F32)
        return (q_ref[:, columns].astype(F32) + delta.astype(BF16).astype(F32)).astype(BF16)

    def put(kind, columns, block):
        if kind == "dv":
            back_ref[:, columns] = block[:ATTENTION_SPAN].astype(BF16)
            dv_ref[:, columns] = block[ATTENTION_SPAN:]
        else:
            (o_ref if kind == "o" else dq_ref)[:, columns] = block

    lane_width = k_ref.shape[1]
    heads_step(
        first_row(rows_dev),
        d_ref[...],
        query_of,
        g_ref,
        lambda lanes: jnp.concatenate([rim_ref[:, lanes], k_ref[:, lanes]], axis=0),
        lambda lanes: jnp.concatenate(
            [rim_ref[:, lane_width + lanes.start : lane_width + lanes.stop], v_ref[:, lanes]],
            axis=0,
        ),
        lane_width // LANES,
        kv_heads,
        group,
        put,
    )


def select(wide, ids, local, rank):
    total = jnp.zeros((rank, ids.shape[1]), F32)
    for j in range(wide.shape[0] // rank):
        total = total + jnp.where(ids == tenant(j, local), wide[j * rank : (j + 1) * rank], 0.0)
    return total


def products_kernel(rank, pieces, local, *refs):
    up_refs, refs = refs[:pieces], refs[pieces:]
    ids_ref, et_ref, dq_ref = refs[:3]
    mine_ref, other_ref, f_ref = refs[3:]
    up = jnp.concatenate([r[...] for r in up_refs], axis=0)
    half = mine_ref.shape[0]
    wide = lax.dot_general(up, dq_ref[...], NT, preferred_element_type=F32)
    f_ref[...] = select(wide, ids_ref[...], local, rank)
    grad = jnp.dot(et_ref[...], dq_ref[...], preferred_element_type=F32).astype(BF16)
    mine_ref[...] = grad[:half]
    other_ref[...] = grad[half:]


def final_kernel(rank, pieces, chunks, local, *refs):
    f_refs, refs = refs[: chunks - 1], refs[chunks - 1 :]
    up_refs, refs = refs[:pieces], refs[pieces:]
    dv_refs, refs = refs[:chunks], refs[chunks:]
    ids_ref, etq_ref, dq_ref, up_ref, etv_ref, edge_ref, back_ref = refs[:7]
    mine_ref, other_ref, mine_v_ref, other_v_ref, f_ref = refs[7:]
    up = jnp.concatenate([r[...] for r in up_refs], axis=0)
    half = mine_ref.shape[0]
    ids = ids_ref[...]
    wide = lax.dot_general(up, dq_ref[...], NT, preferred_element_type=F32)
    factor = select(wide, ids, local, rank)
    for r in f_refs:
        factor = factor + r[...]
    kv_width = mine_v_ref.shape[1]
    total = jnp.concatenate([r[...] for r in dv_refs], axis=1)
    rows = total.shape[0]
    total = jnp.concatenate(
        [
            total[:ATTENTION_SPAN] + edge_ref[...],
            total[ATTENTION_SPAN : rows - ATTENTION_SPAN],
            total[rows - ATTENTION_SPAN :] + back_ref[...].astype(F32),
        ],
        axis=0,
    )
    total = total.astype(BF16)[:, :kv_width]
    wide = lax.dot_general(up_ref[...], total, NT, preferred_element_type=F32)
    f_ref[:rank] = factor
    f_ref[rank:] = select(wide, ids, local, rank)
    grad = jnp.dot(etq_ref[...], dq_ref[...], preferred_element_type=F32).astype(BF16)
    mine_ref[...] = grad[:half]
    other_ref[...] = grad[half:]
    grad = jnp.dot(etv_ref[...], total, preferred_element_type=F32).astype(BF16)
    mine_v_ref[...] = grad[:half]
    other_v_ref[...] = grad[half:]


def outer_kernel(sets, parts, pieces, local, *refs):
    f_refs, refs = refs[: sets * parts], refs[sets * parts :]
    id_refs, refs = refs[:sets], refs[sets:]
    h_refs, out_refs = refs[:sets], refs[sets:]
    total = None
    for n in range(sets):
        factor = f_refs[n * parts][...]
        for k in range(1, parts):
            factor = factor + f_refs[n * parts + k][...]
        ids = id_refs[n][...]
        wide = jnp.concatenate(
            [
                jnp.where(ids == tenant(j, local), factor, 0.0).astype(BF16)
                for j in range(pieces * local)
            ],
            axis=0,
        )
        term = lax.dot_general(wide, h_refs[n][...], NT, preferred_element_type=F32)
        total = term if total is None else total + term
    high = out_refs[0].shape[0]
    for p in range(pieces):
        out_refs[p][...] = total[p * high : (p + 1) * high].astype(BF16)


def body(
    hidden_input,
    query_base,
    frozen_keys,
    frozen_values,
    attended_gradient,
    tenant_ids,
    doc_start,
    a_query,
    b_query,
    a_value,
    value_up_factor,
):
    rows_dev, width = hidden_input.shape
    query_width = query_base.shape[1]
    kv_width = frozen_keys.shape[1]
    local, _, rank = a_query.shape
    both = 2 * rank
    ns, nk, no = lax.axis_size("seq"), lax.axis_size("kvh"), lax.axis_size("own")
    seq_at, own_at = lax.axis_index("seq"), lax.axis_index("own")
    kv_heads = kv_width // HEAD_SIZE
    group = query_width // kv_width
    wide = ns * no * local * rank
    pieces = ns * no
    high = local * rank
    everyone = ("seq", "own")

    def whole(*shape):
        return pl.BlockSpec(shape, lambda i: (0,) * len(shape))

    def call(kernel, name, mebibytes, outs, *operands):
        return pl.pallas_call(
            kernel,
            grid=(1,),
            out_shape=[jax.ShapeDtypeStruct(shape, kind) for shape, kind in outs],
            in_specs=[x[1] if isinstance(x, tuple) else whole(*x.shape) for x in operands],
            out_specs=[whole(*shape) for shape, _ in outs],
            compiler_params=params(mebibytes, dimension_semantics=("arbitrary",)),
            name=name,
        )(*[x[0] if isinstance(x, tuple) else x for x in operands])

    def columns_of(array, p):
        return array, pl.BlockSpec((rows_dev, chunk), lambda i: (0, p))

    def gather_up(block):
        row = [block] + [rotate(block, "seq", k) for k in range(1, ns)]
        return row + [rotate(piece, "own", d) for d in range(1, no) for piece in row]

    value_up = value_up_factor.reshape(high, kv_width)
    value_row = jnp.concatenate(
        [value_up] + [rotate(value_up, "seq", k) for k in range(1, ns)], axis=0
    )
    value_rows = [value_row] + [rotate(value_row, "own", d) for d in range(1, no)]

    a_own = jnp.concatenate([a_query.swapaxes(1, 2), a_value.swapaxes(1, 2)], axis=1).reshape(
        local * both, width
    )
    a_pieces = [a_own] + [rotate(a_own, "seq", k) for k in range(1, ns)]

    hidden_t = hidden_input.T
    ids = tenant_ids.reshape(1, rows_dev)
    hidden_sets = [hidden_t] + [rotate(hidden_t, "own", d) for d in range(1, no)]
    id_sets = [ids] + [rotate(ids, "own", d) for d in range(1, no)]

    pairs = -(-kv_heads // 2)
    chunk = query_width // pairs
    flat = b_query.reshape(high, query_width)
    up_pieces = []
    done = a_pieces
    for p in range(pairs):
        block = after(flat[:, p * chunk : (p + 1) * chunk], *done)
        up_pieces.append(gather_up(block))
        done = up_pieces[-1][:ns]

    code_parts = call(
        lambda *refs: codes_kernel(ns, no, local, *refs),
        "codes",
        16,
        [((both, rows_dev), F32)] * no,
        *a_pieces,
        *hidden_sets,
        *id_sets,
    )

    parts = [code_parts[0]]
    for dk in range(nk):
        for d in range(no):
            if dk or d:
                parts.append(rotate_two(code_parts[(-d) % no], dk, d))

    value_new, rows_q, et_query, et_value, tail, up_value = call(
        lambda *refs: spread_kernel(nk * no, local, *refs),
        "spread",
        12,
        [
            ((rows_dev, kv_width), BF16),
            ((rows_dev, wide), BF16),
            ((wide, rows_dev), BF16),
            ((wide, rows_dev), BF16),
            ((ATTENTION_SPAN, 2 * kv_width), BF16),
            ((wide, kv_width), BF16),
        ],
        *parts,
        value_row,
        value_rows[1] if no == 2 else jnp.concatenate(value_rows[1:], axis=0),
        ids,
        frozen_keys,
        frozen_values,
    )
    rim = shifted(tail, everyone, 1)

    keys, values = frozen_keys, value_new
    lane_gap = (-kv_width) % LANES
    if lane_gap:
        keys = jnp.pad(keys, ((0, 0), (0, lane_gap)))
        values = jnp.pad(values, ((0, 0), (0, lane_gap)))
        rim = jnp.pad(rim.reshape(ATTENTION_SPAN, 2, kv_width), ((0, 0), (0, 0), (0, lane_gap)))
        rim = rim.reshape(ATTENTION_SPAN, 2 * (kv_width + lane_gap))
    lane_width = kv_width + lane_gap
    block = ATTENTION_SPAN
    starts = doc_start.reshape(1, rows_dev)

    def at_rows(columns, place):
        return pl.BlockSpec((block, columns), lambda i: (i + 1, place))

    grads_shape = [jax.ShapeDtypeStruct((rows_dev, query_width), BF16)] * 2
    inner_steps = rows_dev // block - 1

    def inner(p, held):
        return pl.pallas_call(
            lambda *refs: inner_kernel(min(2, kv_heads), group, pieces, len(held), rows_dev, *refs),
            grid=(inner_steps,),
            out_shape=grads_shape + [jax.ShapeDtypeStruct((rows_dev, LANES), F32)],
            in_specs=[whole(high, chunk)] * pieces
            + [
                at_rows(chunk, p),
                at_rows(chunk, p),
                at_rows(wide, 0),
                pl.BlockSpec((rows_dev, LANES), lambda i: (0, p)),
                pl.BlockSpec((rows_dev, LANES), lambda i: (0, p)),
                pl.BlockSpec((1, block), lambda i: (0, i + 1)),
            ]
            + [pl.BlockSpec(memory_space=pl.ANY)] * len(held),
            out_specs=[at_rows(chunk, p), at_rows(chunk, p), whole(rows_dev, LANES)],
            input_output_aliases={6 + pieces + n: n for n in range(len(held))},
            scratch_shapes=[pltpu.VMEM((wide, chunk), BF16)],
            compiler_params=params(20, dimension_semantics=("arbitrary",)),
            name="inner",
        )(*up_pieces[p], query_base, attended_gradient, rows_q, keys, values, starts, *held)

    def reduce_rows(mine, other):
        each = wide // no
        total = mine.astype(F32)
        for d in range(1, no):
            total = total + rotate(other[(d - 1) * each : d * each], "own", -d).astype(F32)
        total = total.astype(BF16).reshape(ns, high, -1)
        result = total[0].astype(F32)
        for k in range(1, ns):
            result = result + rotate(total[k], "seq", -k).astype(F32)
        return result.reshape(local, rank, -1)

    attended, query_grad, dv_first = inner(0, ())
    attended, query_grad, back, dv_edge = pl.pallas_call(
        lambda *refs: edge_kernel(kv_heads, group, pairs, pieces, rows_dev, *refs),
        grid=(1,),
        out_shape=grads_shape
        + [
            jax.ShapeDtypeStruct((block, lane_width), BF16),
            jax.ShapeDtypeStruct((block, lane_width), F32),
        ],
        in_specs=[whole(high, chunk)] * (pieces * pairs)
        + [
            whole(block, query_width),
            whole(block, query_width),
            whole(block, wide),
            whole(block, lane_width),
            whole(block, lane_width),
            whole(block, 2 * lane_width),
            whole(1, block),
            pl.BlockSpec(memory_space=pl.ANY),
            pl.BlockSpec(memory_space=pl.ANY),
        ],
        out_specs=[
            whole(block, query_width),
            whole(block, query_width),
            whole(block, lane_width),
            whole(block, lane_width),
        ],
        input_output_aliases={7 + pieces * pairs: 0, 8 + pieces * pairs: 1},
        compiler_params=params(20, dimension_semantics=("arbitrary",)),
        name="edge",
    )(
        *[piece for row in up_pieces for piece in row],
        query_base,
        attended_gradient,
        rows_q,
        keys,
        values,
        rim,
        starts,
        attended,
        query_grad,
    )
    back = shifted(back, everyone, -1)
    dv_parts = [dv_first]
    f_parts, grad_up = [], []
    half = wide // no
    for p in range(1, pairs):
        mine, other, f_part = call(
            lambda *refs: products_kernel(rank, pieces, local, *refs),
            "products",
            20,
            [((half, chunk), BF16), ((wide - half, chunk), BF16), ((rank, rows_dev), F32)],
            *up_pieces[p - 1],
            ids,
            et_query,
            columns_of(query_grad, p - 1),
        )
        grad_up.append((mine, other))
        f_parts.append(f_part)
        attended, query_grad, dv_next = inner(p, (attended, query_grad))
        dv_parts.append(dv_next)
    mine, other, mine_value, other_value, factor_own = call(
        lambda *refs: final_kernel(rank, pieces, pairs, local, *refs),
        "final",
        24,
        [
            ((half, chunk), BF16),
            ((wide - half, chunk), BF16),
            ((half, kv_width), BF16),
            ((wide - half, kv_width), BF16),
            ((both, rows_dev), F32),
        ],
        *f_parts,
        *up_pieces[-1],
        *dv_parts,
        ids,
        et_query,
        columns_of(query_grad, pairs - 1),
        up_value,
        et_value,
        dv_edge,
        back,
    )
    grad_up.append((mine, other))
    grad_up = [reduce_rows(mine, other) for mine, other in grad_up]
    grad_value = reduce_rows(mine_value, other_value)

    factors = []
    for d in range(no):
        for dk in range(nk):
            factors.append(rotate_two(factor_own, dk, d) if dk or d else factor_own)

    outer_parts = call(
        lambda *refs: outer_kernel(no, nk, ns, local, *refs),
        "outer",
        16,
        [((local * both, width), BF16)] * ns,
        *factors,
        *id_sets,
        *hidden_sets,
    )
    grad_a = outer_parts[0].astype(F32)
    for k in range(1, ns):
        grad_a = grad_a + rotate(outer_parts[k], "seq", -k).astype(F32)
    grad_a = grad_a.reshape(local, both, width)
    return (
        attended,
        grad_a[:, :rank].swapaxes(1, 2),
        jnp.concatenate(grad_up, axis=2),
        grad_a[:, rank:].swapaxes(1, 2),
        grad_value,
    )


def solution(mesh):
    rows = ("grp", "seq", "own")
    in_specs = (
        P(rows, "kvh"),
        P(rows, "kvh"),
        P(rows, "kvh"),
        P(rows, "kvh"),
        P(rows, "kvh"),
        P(rows, None),
        P(rows),
        P(rows, "kvh", None),
        P(rows, None, "kvh"),
        P(rows, "kvh", None),
        P(rows, None, "kvh"),
    )
    out_specs = (
        P(rows, "kvh"),
        P(rows, "kvh", None),
        P(rows, None, "kvh"),
        P(rows, "kvh", None),
        P(rows, None, "kvh"),
    )
    return jax.shard_map(body, mesh=mesh, in_specs=in_specs, out_specs=out_specs, check_vma=False)
```
